128 devices in a mesh: occ: 4 (over x), vir: 32 (over y, z, core).
Axes of the slice: x: 4, y: 4, z: 4, core: 2. Of those that a mesh axis runs over, the one named last changes fastest.
Arguments:
- amplitudes: bfloat16 [256, 262144], P('occ', 'vir'), may hold values from -6 to 6
- cycle_integrals: bfloat16 [16, 64, 16, 64], P(None, None, 'occ'), may hold values from -0.1875 to 0.1875
- ladder_tiles: bfloat16 [2048, 4, 128, 128], P('vir'), may hold values from -0.25 to 0.25
- ladder_rows: int32 [2048, 4], P('vir'), may hold values from 0 to 2047, as said below
- ladder_count: int32 [2048], P('vir'), may hold values from 2 to 4
- row_gap: float32 [256], P('occ'), may hold values from 1 to 3
- column_energy: float32 [262144], P('vir'), may hold values from 0.5 to 8
Outputs:
- updated: bfloat16 [256, 262144], P('occ', 'vir')
The draws below stay inside these ranges and needn't reach their ends.
Inputs may be any that keep to these rules, and one draw needn't show every extreme that they name: `ladder_rows`: each entry of column tile c's list names a virtual-pair tile within 2 tiles of c; entry 0 is max(c - 2, 0) and entry 1 is min(c + 2, 2047).
All inputs are finite; a program needn't handle non-finite values.
Results may differ from the reference program's by a relative error of at most 0.0019.
Values may be sent and summed in bfloat16 or wider, within the bound.
A program may use at most 192 MiB of HBM per device.

```python
import math
import jax
import jax.numpy as jnp
from jax import lax

TILE = 128
NJ = 16
NA = 4096
KMAX = 4
HT = 2
NI = 16
NB = 64
ROWS = 256
COLS = 262144
CTT = 2048


def draw_ladder_rows(key, part):
    shifts = jax.random.randint(key, (CTT, KMAX), -HT, HT + 1).astype(jnp.int32)
    entry = jnp.arange(KMAX, dtype=jnp.int32)[None, :]
    shifts = jnp.where(entry == 0, -HT, jnp.where(entry == 1, HT, shifts)).astype(jnp.int32)
    column_tiles = jnp.arange(CTT, dtype=jnp.int32)[:, None]
    return jnp.clip(column_tiles + shifts, 0, CTT - 1).astype(jnp.int32)


def set_ends(array, rng, smallest, high):
    place = [jax.random.randint(jax.random.fold_in(rng, axis), (), 0, length) for axis, length in enumerate(array.shape)]
    longest = array.shape.index(max(array.shape))
    next_to = place[:longest] + [(place[longest] + 1) % array.shape[longest]] + place[longest + 1:]
    return array.at[tuple(place)].set(smallest).at[tuple(next_to)].set(high)


def levels(key, shape, shards, least, top_value):
    def one(position, blocks):
        heights = jax.random.uniform(jax.random.fold_in(jax.random.fold_in(key, 6), position), (blocks,), jnp.float32, least / len(shards), top_value / len(shards))
        return jnp.repeat(jnp.exp(heights), shape[position] // blocks).reshape((-1,) + (1,) * (len(shape) - position - 1))

    level = one(*shards[0])
    for cut in shards[1:]:
        level = level * one(*cut)
    return level


def scatter_about(stream_key, shape, spread, limit, split=(), held_as=jnp.bfloat16):
    loudness = levels(stream_key, shape, split, -0.22, 0.18) if split else 1.0
    values = jax.random.normal(stream_key, shape, jnp.float32) * spread * loudness
    return jnp.minimum(jnp.maximum(values, -limit), limit).astype(held_as)


def setup_inputs(seed: int = 0) -> dict:
    keys = jax.random.split(jax.random.key(seed), 8)
    amplitudes = scatter_about(keys[0], (ROWS, COLS), 1.0, 6.0, ((0, 4), (1, 32)))
    cycle_integrals = scatter_about(keys[1], (NJ, NB, NJ, NB), (NJ * NB) ** -0.5, 0.1875, ((2, 4),))
    ladder_tiles = scatter_about(keys[2], (CTT, KMAX, TILE, TILE), (KMAX * TILE) ** -0.5, 0.25, ((0, 32),))
    ladder_rows = draw_ladder_rows(jax.random.fold_in(keys[7], 71), 0)
    ladder_count = set_ends(jax.random.randint(keys[4], (CTT,), 2, KMAX + 1), jax.random.fold_in(keys[4], 1), 2, KMAX).astype(jnp.int32)
    row_gap = jnp.clip(1.0 + 2.0 * jax.random.uniform(keys[5], (ROWS,), jnp.float32) ** levels(keys[5], (ROWS,), ((0, 4),), -0.2, 0.2), 1.0, 3.0)
    column_energy = jnp.clip(jnp.exp(math.log(8.0) - 2.7725887 * jax.random.uniform(keys[6], (COLS,), jnp.float32) ** levels(keys[6], (COLS,), ((0, 32),), -0.2, 0.2)), 0.5, 8.0)
    return {"amplitudes": amplitudes, "cycle_integrals": cycle_integrals, "ladder_tiles": ladder_tiles, "ladder_rows": ladder_rows, "ladder_count": ladder_count, "row_gap": row_gap, "column_energy": column_energy}


def reference(amplitudes, cycle_integrals, ladder_tiles, ladder_rows, ladder_count, row_gap, column_energy):
    cycle_float = cycle_integrals.astype(jnp.float32)
    blocks = amplitudes.reshape(NI, NJ, NB, NA)

    def cycle_block(amp_block):
        return jnp.einsum('jba,jbkc->kca', amp_block.astype(jnp.float32), cycle_float).astype(jnp.bfloat16)

    cycle = lax.map(cycle_block, blocks).reshape(ROWS, COLS)
    tiled = amplitudes.reshape(ROWS, CTT, TILE)

    def tile_update(inputs):
        tile_index, rows_list, count_one, tiles_one = inputs
        picked = jnp.take(tiled, rows_list, axis=1)
        live_mask = jnp.arange(KMAX, dtype=jnp.int32) < count_one
        live_tiles = jnp.where(live_mask[:, None, None], tiles_one, jnp.zeros((), jnp.bfloat16))
        ladder = jnp.einsum('rkp,kpq->rq', picked.astype(jnp.float32), live_tiles.astype(jnp.float32))
        offset = (tile_index * TILE).astype(jnp.int32)
        cycle_part = lax.dynamic_slice_in_dim(cycle, offset, TILE, 1)
        old_part = lax.dynamic_slice_in_dim(amplitudes, offset, TILE, 1)
        energy = lax.dynamic_slice_in_dim(column_energy, offset, TILE, 0)
        denominator = row_gap[:, None] + energy[None, :]
        return (old_part.astype(jnp.float32) + (cycle_part.astype(jnp.float32) + ladder) / denominator).astype(jnp.bfloat16)

    result = lax.map(tile_update, (jnp.arange(CTT, dtype=jnp.int32), ladder_rows, ladder_count, ladder_tiles))
    return jnp.transpose(result, (1, 0, 2)).reshape(ROWS, COLS)
```

```python
import functools
import itertools

import jax
import jax.numpy as jnp
from jax import lax
from jax.experimental import pallas as pl
from jax.experimental.pallas import tpu as pltpu
from jax.sharding import PartitionSpec as P

TILE = 128
NJ = 16
NA = 4096
NB_DEV = 2
KMAX = 4
HT = 2
MESH = pl.DeviceIdType.MESH

STEPS = sorted(
    (d for d in itertools.product(range(4), range(4), range(2)) if any(d)),
    key=lambda d: -(min(d[0], 4 - d[0]) + min(d[1], 4 - d[1])),
)


def kernel(
    rows_ref, count_ref, amp_ref, integrals_ref, tiles_ref, gap_ref, energy_ref, out_ref,
    amp, blocks, weights, tiles, made, cycle, base, scale,
    in_send, in_recv, w_send, w_recv, f_send, f_recv, out_send, out_recv,
    halo_send, halo_recv, local_sem,
):
    occ, vir = lax.axis_index("occ"), lax.axis_index("vir")
    y, z, core = vir // 8, (vir // 2) % 4, vir % 2
    rows_dev = amp_ref.shape[0]
    cols_dev = amp_ref.shape[1]
    tiles_dev = cols_dev // TILE
    halo = HT * TILE

    def partner(d):
        return (((y + d[0]) % 4) * 4 + (z + d[1]) % 4) * 2 + (core + d[2]) % 2

    def source(d):
        return (((y + 4 - d[0]) % 4) * 4 + (z + 4 - d[1]) % 4) * 2 + (core + d[2]) % 2

    def lanes(start, size):
        return pl.ds(pl.multiple_of(start, TILE), size)

    get_amp = pltpu.make_async_copy(amp_ref, amp.at[:, pl.ds(halo, cols_dev)], local_sem.at[0])
    get_own = pltpu.make_async_copy(integrals_ref, weights.at[occ], local_sem.at[1])
    get_tiles = pltpu.make_async_copy(tiles_ref, tiles, local_sem.at[2])
    get_amp.start()
    get_own.start()

    barrier = pltpu.get_barrier_semaphore()
    for d in STEPS:
        pl.semaphore_signal(barrier, inc=1, device_id=(occ, partner(d)), device_id_type=MESH)
    for s in (2, 1, 3):
        pl.semaphore_signal(barrier, inc=1, device_id=((occ + s) % 4, vir), device_id_type=MESH)
    get_tiles.start()
    pl.semaphore_wait(barrier, len(STEPS) + 3)

    half = weights.shape[1] // 2
    mine = pl.ds(pl.multiple_of(core * half, half), half)
    w_copies = []
    get_own.wait()
    for n, s in enumerate((1, 3, 2)):
        w_copies.append(pltpu.make_async_remote_copy(
            weights.at[occ, mine], weights.at[occ, mine], w_send.at[n], w_recv.at[n],
            device_id=((occ + s) % 4, vir), device_id_type=MESH,
        ))
        w_copies[-1].start()

    own_in = []
    for b in range(NB_DEV):
        own_in.append(pltpu.make_async_copy(
            amp_ref.at[:, lanes(b * NA + vir * TILE, TILE)], blocks.at[vir, b], in_recv
        ))
        own_in[-1].start()
    for d in STEPS:
        u = partner(d)
        for b in range(NB_DEV):
            pltpu.make_async_remote_copy(
                amp_ref.at[:, lanes(b * NA + u * TILE, TILE)], blocks.at[vir, b], in_send, in_recv,
                device_id=(occ, u), device_id_type=MESH,
            ).start()

    get_amp.wait()
    up = pltpu.make_async_remote_copy(
        amp.at[:, pl.ds(cols_dev, halo)], amp.at[:, pl.ds(0, halo)], halo_send.at[0], halo_recv.at[0],
        device_id=(occ, (vir + 1) % 32), device_id_type=MESH,
    )
    down = pltpu.make_async_remote_copy(
        amp.at[:, pl.ds(halo, halo)], amp.at[:, pl.ds(halo + cols_dev, halo)], halo_send.at[1],
        halo_recv.at[1], device_id=(occ, (vir + 31) % 32), device_id_type=MESH,
    )
    up.start()
    down.start()

    gap_row = jnp.broadcast_to(gap_ref[...], (rows_dev, rows_dev))
    on_diagonal = lax.broadcasted_iota(jnp.int32, (rows_dev, rows_dev), 0) == lax.broadcasted_iota(
        jnp.int32, (rows_dev, rows_dev), 1
    )
    gap = jnp.sum(jnp.where(on_diagonal, gap_row, 0.0), axis=1, keepdims=True)
    gap = jnp.broadcast_to(gap, (rows_dev, TILE))

    up.wait()
    down.wait()
    get_tiles.wait()
    first_tile = vir * tiles_dev - HT

    def ladder_step(c, carry):
        near = [amp[:, lanes((c + q) * TILE, TILE)] for q in range(2 * HT + 1)]
        tile = vir * tiles_dev + c
        at = (jnp.maximum(tile - HT, 0) - first_tile, jnp.minimum(tile + HT, 32 * tiles_dev - 1) - first_tile)
        picked = [amp[:, lanes(a * TILE, TILE)] for a in at]
        for k in range(2, KMAX):
            offset = rows_ref[k, c] - (tile - HT)
            one = near[0]
            for q in range(1, 2 * HT + 1):
                one = jnp.where(offset == q, near[q], one)
            picked.append(jnp.where(count_ref[c] > k, one, jnp.zeros_like(one)))
        term = jnp.dot(
            jnp.concatenate(picked, axis=1), tiles[c].reshape(KMAX * TILE, TILE),
            preferred_element_type=jnp.float32,
        )
        inverse = 1.0 / (gap + energy_ref[pl.ds(c, 1), :])
        old = amp[:, lanes(halo + c * TILE, TILE)].astype(jnp.float32)
        scale[c] = inverse
        base[c] = old + term * inverse
        return carry

    lax.fori_loop(0, tiles_dev, ladder_step, 0)

    forwards = []
    for n, s in enumerate((1, 3, 2)):
        w_copies[n].wait()
        part = weights.at[(occ + 4 - s) % 4, mine]
        forwards.append(pltpu.make_async_remote_copy(
            part, part, f_send.at[n], f_recv.at[n],
            device_id=(occ, partner((0, 0, 1))), device_id_type=MESH,
        ))
        forwards[-1].start()

    pltpu.make_async_copy(blocks, blocks, in_recv).wait()

    own_out = []
    for n, s in enumerate((0, 1, 3, 2)):
        o = (occ + 4 - s) % 4
        if s:
            forwards[n - 1].wait()
        w = weights[o]
        for p in range(2):
            rhs = jnp.concatenate(
                [blocks[:, :, pl.ds(i * NJ, NJ), :].reshape(-1, TILE) for i in (2 * p, 2 * p + 1)],
                axis=1,
            )
            part = jnp.dot(w, rhs, preferred_element_type=jnp.float32)
            pair = [part[:, i * TILE:(i + 1) * TILE].reshape(32, 8, TILE) for i in range(2)]
            made[o, :, p] = jnp.concatenate(pair, axis=1).astype(jnp.bfloat16)
        own_out.append(pltpu.make_async_copy(made.at[o, vir], cycle.at[vir, o], out_recv.at[len(STEPS)]))
        own_out[-1].start()
        for q, d in enumerate(STEPS):
            u = partner(d)
            pltpu.make_async_remote_copy(
                made.at[o, u], cycle.at[vir, o], out_send, out_recv.at[q],
                device_id=(occ, u), device_id_type=MESH,
            ).start()

    low = lax.broadcasted_iota(jnp.int32, (2, 4, 8, TILE), 2) < 4
    for q, d in enumerate(STEPS + [(0, 0, 0)]):
        v = source(d)
        pltpu.make_async_copy(cycle.at[v], cycle.at[v], out_recv.at[q]).wait()
        got = cycle[v].astype(jnp.float32).reshape(2, 2, 4, 8, TILE)
        even, odd = got[:, 0], got[:, 1]
        for b in range(NB_DEV):
            if b == 0:
                term = jnp.where(low, even, pltpu.roll(odd, 4, 2))
            else:
                term = jnp.where(low, pltpu.roll(even, 4, 2), odd)
            term = jnp.transpose(term, (1, 0, 2, 3)).reshape(rows_dev, TILE)
            c = b * (NA // TILE) + v
            out_ref[:, lanes(c * TILE, TILE)] = (base[c] + term * scale[c]).astype(jnp.bfloat16)

    sent = blocks.at[pl.ds(0, len(STEPS))]
    pltpu.make_async_copy(sent, sent, in_send).wait()
    sent = cycle.at[pl.ds(0, len(STEPS))]
    pltpu.make_async_copy(sent, sent, out_send).wait()


def local(
    amplitudes, cycle_integrals, ladder_tiles, ladder_rows, ladder_count, row_gap, column_energy
):
    rows_dev, cols_dev = amplitudes.shape
    tiles_dev = cols_dev // TILE
    integrals = jnp.transpose(cycle_integrals, (3, 2, 1, 0)).reshape(256, 1024)
    bf16, f32 = jnp.bfloat16, jnp.float32
    dma = pltpu.SemaphoreType.DMA
    any_space = pl.BlockSpec(memory_space=pl.ANY)
    smem, vmem = pl.BlockSpec(memory_space=pltpu.SMEM), pl.BlockSpec(memory_space=pltpu.VMEM)
    return pl.pallas_call(
        kernel,
        out_shape=jax.ShapeDtypeStruct((rows_dev, cols_dev), bf16),
        in_specs=[smem, smem, any_space, any_space, any_space, vmem, vmem],
        out_specs=vmem,
        scratch_shapes=[
            pltpu.VMEM((rows_dev, cols_dev + 2 * HT * TILE), bf16),
            pltpu.VMEM((32, NB_DEV, rows_dev, TILE), bf16),
            pltpu.VMEM((4, 256, 1024), bf16),
            pltpu.VMEM((tiles_dev, KMAX, TILE, TILE), bf16),
            pltpu.VMEM((4, 32, 2, 16, TILE), bf16),
            pltpu.VMEM((32, 4, 2, 16, TILE), bf16),
            pltpu.VMEM((tiles_dev, rows_dev, TILE), f32),
            pltpu.VMEM((tiles_dev, rows_dev, TILE), f32),
            dma, dma, dma((3,)), dma((3,)), dma((3,)), dma((3,)), dma, dma((32,)),
            dma((2,)), dma((2,)), dma((3,)),
        ],
        compiler_params=pltpu.CompilerParams(
            collective_id=0, has_side_effects=True, vmem_limit_bytes=48 * 2**20
        ),
        name="cycle_and_ladder",
    )(
        ladder_rows.T, ladder_count, amplitudes, integrals, ladder_tiles,
        row_gap.reshape(1, rows_dev), column_energy.reshape(tiles_dev, TILE),
    )


def solution(mesh):
    in_specs = (
        P("occ", "vir"),
        P(None, None, "occ", None),
        P("vir", None, None, None),
        P("vir", None),
        P("vir"),
        P("occ"),
        P("vir"),
    )
    return jax.shard_map(
        local, mesh=mesh, in_specs=in_specs, out_specs=P("occ", "vir"), check_vma=False
    )
```

```python
import functools
import itertools

import jax
import jax.numpy as jnp
from jax import lax
from jax.experimental import pallas as pl
from jax.experimental.pallas import tpu as pltpu
from jax.sharding import PartitionSpec as P

TILE = 128
NJ = 16
NA = 4096
NB_DEV = 2
KMAX = 4
HT = 2
MESH = pl.DeviceIdType.MESH

PARTS = 2
EARLY = 8
UNROLL = 8
TURNS = (0, 1, 3, 2)

STEPS = sorted(
    (d for d in itertools.product(range(4), range(4), range(2)) if any(d)),
    key=lambda d: -(min(d[0], 4 - d[0]) + min(d[1], 4 - d[1])),
)


def kernel(
    rows_ref, count_ref, amp_ref, integrals_ref, tiles_ref, gap_ref, energy_ref, out_ref,
    amp, blocks, weights, tiles, made, cycle, base, scale, raw, spread, gap_row, energy, rows, count,
    in_send, in_recv, w_send, w_recv, f_send, f_recv, out_send, out_recv,
    halo_send, halo_recv, local_sem,
):
    occ, vir = lax.axis_index("occ"), lax.axis_index("vir")
    y, z, core = vir // 8, (vir // 2) % 4, vir % 2
    rows_dev = amp_ref.shape[0]
    cols_dev = amp_ref.shape[1]
    tiles_dev = cols_dev // TILE
    halo = HT * TILE
    part_rows = rows_dev // PARTS

    def partner(d):
        return (((y + d[0]) % 4) * 4 + (z + d[1]) % 4) * 2 + (core + d[2]) % 2

    def source(d):
        return (((y + 4 - d[0]) % 4) * 4 + (z + 4 - d[1]) % 4) * 2 + (core + d[2]) % 2

    def lanes(start, size):
        return pl.ds(pl.multiple_of(start, TILE), size)

    get_amp = pltpu.make_async_copy(amp_ref, amp.at[:, pl.ds(halo, cols_dev)], local_sem.at[0])
    get_own = pltpu.make_async_copy(integrals_ref, raw, local_sem.at[1])
    get_tiles = pltpu.make_async_copy(tiles_ref, tiles, local_sem.at[2])
    get_small = [
        pltpu.make_async_copy(a, b, local_sem.at[3 + n])
        for n, (a, b) in enumerate(
            ((gap_ref, gap_row), (energy_ref, energy), (rows_ref, rows), (count_ref, count))
        )
    ]
    get_own.start()

    barrier = pltpu.get_barrier_semaphore()
    for d in STEPS:
        pl.semaphore_signal(barrier, inc=1, device_id=(occ, partner(d)), device_id_type=MESH)
    for s in (2, 1, 3):
        pl.semaphore_signal(barrier, inc=1, device_id=((occ + s) % 4, vir), device_id_type=MESH)
    get_amp.start()
    for g in get_small:
        g.start()
    get_tiles.start()

    get_own.wait()
    spread[...] = raw[...].astype(jnp.float32)
    nb = raw.shape[1]
    n_low = raw.shape[0] // (NJ * nb)
    group = 16
    row = lax.broadcasted_iota(jnp.int32, (nb * n_low, nb), 0)
    column = lax.broadcasted_iota(jnp.int32, (nb * n_low, nb), 1)

    def turn(g, carry):
        total = jnp.zeros((nb * n_low, group * NJ), jnp.float32)
        for j2 in range(n_low):
            one = [
                spread[pl.ds((g * group + b) * n_low + j2, NJ, stride=nb * n_low), :]
                for b in range(group)
            ]
            place = jnp.where(row == column * n_low + j2, 1.0, 0.0).astype(jnp.bfloat16)
            total += lax.dot_general(
                place, jnp.concatenate(one, axis=0).astype(jnp.bfloat16), (((1,), (1,)), ((), ())),
                preferred_element_type=jnp.float32,
            )
        weights[occ, :, lanes(g * group * NJ, group * NJ)] = total.astype(jnp.bfloat16)
        return carry

    lax.fori_loop(0, nb // group, turn, 0)
    pl.semaphore_wait(barrier, len(STEPS) + 3)

    half = weights.shape[1] // 2
    mine = pl.ds(pl.multiple_of(core * half, half), half)
    w_copies = []
    for n, s in enumerate(TURNS[1:]):
        w_copies.append(pltpu.make_async_remote_copy(
            weights.at[occ, mine], weights.at[occ, mine], w_send.at[n], w_recv.at[n],
            device_id=((occ + s) % 4, vir), device_id_type=MESH,
        ))
        w_copies[-1].start()

    for p in range(PARTS):
        some = pl.ds(p * part_rows, part_rows)
        for d in STEPS:
            u = partner(d)
            for b in range(NB_DEV):
                pltpu.make_async_remote_copy(
                    amp_ref.at[some, lanes(b * NA + u * TILE, TILE)], blocks.at[p, vir, b],
                    in_send, in_recv.at[p], device_id=(occ, u), device_id_type=MESH,
                ).start()
        for b in range(NB_DEV):
            pltpu.make_async_copy(
                amp_ref.at[some, lanes(b * NA + vir * TILE, TILE)], blocks.at[p, vir, b], in_recv.at[p]
            ).start()
        if p == 0:
            get_amp.wait()
            up = pltpu.make_async_remote_copy(
                amp.at[:, pl.ds(cols_dev, halo)], amp.at[:, pl.ds(0, halo)], halo_send.at[0],
                halo_recv.at[0], device_id=(occ, (vir + 1) % 32), device_id_type=MESH,
            )
            down = pltpu.make_async_remote_copy(
                amp.at[:, pl.ds(halo, halo)], amp.at[:, pl.ds(halo + cols_dev, halo)], halo_send.at[1],
                halo_recv.at[1], device_id=(occ, (vir + 31) % 32), device_id_type=MESH,
            )
            up.start()
            down.start()

    for g in get_small:
        g.wait()
    on_diagonal = lax.broadcasted_iota(jnp.int32, (rows_dev, rows_dev), 0) == lax.broadcasted_iota(
        jnp.int32, (rows_dev, rows_dev), 1
    )
    gaps = jnp.broadcast_to(gap_row[...], (rows_dev, rows_dev))
    gap = jnp.sum(jnp.where(on_diagonal, gaps, 0.0), axis=1, keepdims=True)
    gap = jnp.broadcast_to(gap, (rows_dev, TILE))

    up.wait()
    down.wait()
    get_tiles.wait()
    first_tile = vir * tiles_dev - HT

    def ladder_step(c, carry):
        near = [amp[:, lanes((c + q) * TILE, TILE)] for q in range(2 * HT + 1)]
        tile = vir * tiles_dev + c
        at = (jnp.maximum(tile - HT, 0) - first_tile, jnp.minimum(tile + HT, 32 * tiles_dev - 1) - first_tile)
        picked = [amp[:, lanes(a * TILE, TILE)] for a in at]
        for k in range(2, KMAX):
            offset = rows[k, c] - (tile - HT)
            one = near[0]
            for q in range(1, 2 * HT + 1):
                one = jnp.where(offset == q, near[q], one)
            picked.append(jnp.where(count[c] > k, one, jnp.zeros_like(one)))
        term = jnp.dot(
            jnp.concatenate(picked, axis=1), tiles[c].reshape(KMAX * TILE, TILE),
            preferred_element_type=jnp.float32,
        )
        inverse = 1.0 / (gap + energy[pl.ds(c, 1), :])
        old = amp[:, lanes(halo + c * TILE, TILE)].astype(jnp.float32)
        scale[c] = inverse
        base[c] = old + term * inverse
        return carry

    lax.fori_loop(0, EARLY, ladder_step, 0, unroll=UNROLL)

    forwards = []

    def forward(n):
        w_copies[n].wait()
        part = weights.at[(occ + 4 - TURNS[n + 1]) % 4, mine]
        forwards.append(pltpu.make_async_remote_copy(
            part, part, f_send.at[n], f_recv.at[n],
            device_id=(occ, partner((0, 0, 1))), device_id_type=MESH,
        ))
        forwards[-1].start()

    def product(p, n):
        w = weights[(occ + 4 - TURNS[n]) % 4]
        rhs = jnp.concatenate(
            [blocks[p, :, :, pl.ds(i * NJ, NJ), :].reshape(-1, TILE) for i in range(2)], axis=1
        )
        part = jnp.dot(w, rhs, preferred_element_type=jnp.float32)
        pair = [part[:, i * TILE:(i + 1) * TILE].reshape(32, 8, TILE) for i in range(2)]
        made[:, p, n] = jnp.concatenate(pair, axis=1).astype(jnp.bfloat16)

    def send(p, n, size):
        some = pl.ds(n, size)
        pltpu.make_async_copy(
            made.at[vir, p, some], cycle.at[vir, p, some], out_recv.at[len(STEPS)]
        ).start()
        for q, d in enumerate(STEPS):
            u = partner(d)
            pltpu.make_async_remote_copy(
                made.at[u, p, some], cycle.at[vir, p, some], out_send, out_recv.at[q],
                device_id=(occ, u), device_id_type=MESH,
            ).start()

    forward(0)
    forward(1)
    pltpu.make_async_copy(blocks.at[0], blocks.at[0], in_recv.at[0]).wait()
    product(0, 0)
    forwards[0].wait()
    product(0, 1)
    send(0, 0, 2)
    forward(2)
    pltpu.make_async_copy(blocks.at[1], blocks.at[1], in_recv.at[1]).wait()
    product(1, 0)
    product(1, 1)
    send(1, 0, 2)
    forwards[1].wait()
    forwards[2].wait()
    for p in range(PARTS):
        product(p, 2)
        product(p, 3)
        send(p, 2, 2)

    lax.fori_loop(EARLY, tiles_dev, ladder_step, 0, unroll=UNROLL)

    low = lax.broadcasted_iota(jnp.int32, (4, 8, TILE), 1) < 4
    places = []
    for o in range(4):
        s = (occ + 4 - o) % 4
        places.append(s + (s // 2) * (5 - 2 * s))
    for q, d in enumerate(STEPS + [(0, 0, 0)]):
        v = source(d)
        pltpu.make_async_copy(cycle.at[v], cycle.at[v], out_recv.at[q]).wait()
        got = [cycle[v, :, n].astype(jnp.float32).reshape(4, 8, TILE) for n in places]
        for b in range(NB_DEV):
            term = []
            for even, odd in ((got[0], got[1]), (got[2], got[3])):
                if b == 0:
                    term.append(jnp.where(low, even, pltpu.roll(odd, 4, 1)))
                else:
                    term.append(jnp.where(low, pltpu.roll(even, 4, 1), odd))
            term = jnp.stack(term, axis=1).reshape(rows_dev, TILE)
            c = b * (NA // TILE) + v
            out_ref[:, lanes(c * TILE, TILE)] = (base[c] + term * scale[c]).astype(jnp.bfloat16)

    sent = blocks.at[:, pl.ds(0, len(STEPS))]
    pltpu.make_async_copy(sent, sent, in_send).wait()
    sent = cycle.at[pl.ds(0, len(STEPS))]
    pltpu.make_async_copy(sent, sent, out_send).wait()


def local(
    amplitudes, cycle_integrals, ladder_tiles, ladder_rows, ladder_count, row_gap, column_energy
):
    rows_dev, cols_dev = amplitudes.shape
    tiles_dev = cols_dev // TILE
    integrals = cycle_integrals.reshape(-1, cycle_integrals.shape[-1])
    bf16, f32 = jnp.bfloat16, jnp.float32
    dma = pltpu.SemaphoreType.DMA
    hbm, vmem = pl.BlockSpec(memory_space=pltpu.HBM), pl.BlockSpec(memory_space=pltpu.VMEM)
    return pl.pallas_call(
        kernel,
        out_shape=jax.ShapeDtypeStruct((rows_dev, cols_dev), bf16),
        in_specs=[hbm] * 7,
        out_specs=vmem,
        scratch_shapes=[
            pltpu.VMEM((rows_dev, cols_dev + 2 * HT * TILE), bf16),
            pltpu.VMEM((PARTS, 32, NB_DEV, rows_dev // PARTS, TILE), bf16),
            pltpu.VMEM((4, 256, 1024), bf16),
            pltpu.VMEM((tiles_dev, KMAX, TILE, TILE), bf16),
            pltpu.VMEM((32, PARTS, 4, 16, TILE), bf16),
            pltpu.VMEM((32, PARTS, 4, 16, TILE), bf16),
            pltpu.VMEM((tiles_dev, rows_dev, TILE), f32),
            pltpu.VMEM((tiles_dev, rows_dev, TILE), f32),
            pltpu.VMEM(integrals.shape, bf16),
            pltpu.VMEM(integrals.shape, f32),
            pltpu.VMEM((1, rows_dev), f32),
            pltpu.VMEM((tiles_dev, TILE), f32),
            pltpu.SMEM((KMAX, tiles_dev), jnp.int32),
            pltpu.SMEM((tiles_dev,), jnp.int32),
            dma, dma((PARTS,)), dma((3,)), dma((3,)), dma((3,)), dma((3,)), dma, dma((32,)),
            dma((2,)), dma((2,)), dma((7,)),
        ],
        compiler_params=pltpu.CompilerParams(
            collective_id=0, has_side_effects=True, vmem_limit_bytes=62 * 2**20
        ),
        name="cycle_and_ladder",
    )(
        ladder_rows.T, ladder_count, amplitudes, integrals, ladder_tiles,
        row_gap.reshape(1, rows_dev), column_energy.reshape(tiles_dev, TILE),
    )


def solution(mesh):
    in_specs = (
        P("occ", "vir"),
        P(None, None, "occ", None),
        P("vir", None, None, None),
        P("vir", None),
        P("vir"),
        P("occ"),
        P("vir"),
    )
    return jax.shard_map(
        local, mesh=mesh, in_specs=in_specs, out_specs=P("occ", "vir"), check_vma=False
    )
```

```python
import functools
import itertools

import jax
import jax.numpy as jnp
from jax import lax
from jax.experimental import pallas as pl
from jax.experimental.pallas import tpu as pltpu
from jax.sharding import PartitionSpec as P

TILE = 128
NJ = 16
NA = 4096
NB_DEV = 2
KMAX = 4
HT = 2
MESH = pl.DeviceIdType.MESH

PARTS = 2
EARLY = 0
MIDDLE = 0
UNROLL = 8
TURNS = (0, 1, 3, 2)

STEPS = sorted(
    (d for d in itertools.product(range(4), range(4), range(2)) if any(d)),
    key=lambda d: -(min(d[0], 4 - d[0]) + min(d[1], 4 - d[1])),
)


def kernel(
    rows_ref, count_ref, amp_ref, integrals_ref, tiles_ref, gap_ref, energy_ref, out_ref,
    amp, blocks, weights, tiles, made, cycle, base, scale, raw, spread, gap_row, energy, rows, count, result,
    in_send, in_recv, w_send, w_recv, f_send, f_recv, out_send, out_recv,
    halo_send, halo_recv, local_sem,
):
    occ, vir = lax.axis_index("occ"), lax.axis_index("vir")
    y, z, core = vir // 8, (vir // 2) % 4, vir % 2
    rows_dev = amp_ref.shape[0]
    cols_dev = amp_ref.shape[1]
    tiles_dev = cols_dev // TILE
    halo = HT * TILE
    part_rows = rows_dev // PARTS

    def partner(d):
        return (((y + d[0]) % 4) * 4 + (z + d[1]) % 4) * 2 + (core + d[2]) % 2

    def source(d):
        return (((y + 4 - d[0]) % 4) * 4 + (z + 4 - d[1]) % 4) * 2 + (core + d[2]) % 2

    def lanes(start, size):
        return pl.ds(pl.multiple_of(start, TILE), size)

    get_amp = pltpu.make_async_copy(amp_ref, amp.at[:, pl.ds(halo, cols_dev)], local_sem.at[0])
    get_own = pltpu.make_async_copy(integrals_ref, raw, local_sem.at[1])
    get_tiles = pltpu.make_async_copy(tiles_ref, tiles, local_sem.at[2])
    get_small = [
        pltpu.make_async_copy(a, b, local_sem.at[3 + n])
        for n, (a, b) in enumerate(
            ((gap_ref, gap_row), (energy_ref, energy), (rows_ref, rows), (count_ref, count))
        )
    ]
    get_own.start()

    barrier = pltpu.get_barrier_semaphore()
    for d in STEPS:
        pl.semaphore_signal(barrier, inc=1, device_id=(occ, partner(d)), device_id_type=MESH)
    for s in (2, 1, 3):
        pl.semaphore_signal(barrier, inc=1, device_id=((occ + s) % 4, vir), device_id_type=MESH)
    get_amp.start()
    for g in get_small:
        g.start()
    get_tiles.start()

    get_own.wait()
    spread[...] = raw[...].astype(jnp.float32)
    nb = raw.shape[1]
    n_low = raw.shape[0] // (NJ * nb)
    group = 16
    row = lax.broadcasted_iota(jnp.int32, (nb * n_low, nb), 0)
    column = lax.broadcasted_iota(jnp.int32, (nb * n_low, nb), 1)

    def turn(g, carry):
        total = jnp.zeros((nb * n_low, group * NJ), jnp.float32)
        for j2 in range(n_low):
            one = [
                spread[pl.ds((g * group + b) * n_low + j2, NJ, stride=nb * n_low), :]
                for b in range(group)
            ]
            place = jnp.where(row == column * n_low + j2, 1.0, 0.0).astype(jnp.bfloat16)
            total += lax.dot_general(
                place, jnp.concatenate(one, axis=0).astype(jnp.bfloat16), (((1,), (1,)), ((), ())),
                preferred_element_type=jnp.float32,
            )
        weights[occ, :, lanes(g * group * NJ, group * NJ)] = total.astype(jnp.bfloat16)
        return carry

    lax.fori_loop(0, nb // group, turn, 0)
    pl.semaphore_wait(barrier, len(STEPS) + 3)

    half = weights.shape[1] // 2
    mine = pl.ds(pl.multiple_of(core * half, half), half)
    quarter = half // 2
    quarters = [pl.ds(pl.multiple_of(core * half + n * quarter, quarter), quarter) for n in range(2)]
    after, before, across = (occ + 1) % 4, (occ + 3) % 4, (occ + 2) % 4

    def along(slot, some, n, to):
        part = weights.at[slot, some]
        return pltpu.make_async_remote_copy(
            part, part, w_send.at[n], w_recv.at[n], device_id=(to, vir), device_id_type=MESH
        )

    w_copies = [along(occ, mine, 0, after), along(occ, mine, 1, before)]
    for w_copy in w_copies:
        w_copy.start()

    get_amp.wait()
    for p in range(PARTS):
        some = pl.ds(p * part_rows, part_rows)
        for d in STEPS:
            u = partner(d)
            for b in range(NB_DEV):
                pltpu.make_async_remote_copy(
                    amp.at[some, lanes(halo + b * NA + u * TILE, TILE)], blocks.at[p, vir, b],
                    in_send, in_recv.at[p], device_id=(occ, u), device_id_type=MESH,
                ).start()
        for b in range(NB_DEV):
            pltpu.make_async_copy(
                amp_ref.at[some, lanes(b * NA + vir * TILE, TILE)], blocks.at[p, vir, b], in_recv.at[p]
            ).start()
        if p == 0:
            up = pltpu.make_async_remote_copy(
                amp.at[:, pl.ds(cols_dev, halo)], amp.at[:, pl.ds(0, halo)], halo_send.at[0],
                halo_recv.at[0], device_id=(occ, (vir + 1) % 32), device_id_type=MESH,
            )
            down = pltpu.make_async_remote_copy(
                amp.at[:, pl.ds(halo, halo)], amp.at[:, pl.ds(halo + cols_dev, halo)], halo_send.at[1],
                halo_recv.at[1], device_id=(occ, (vir + 31) % 32), device_id_type=MESH,
            )
            up.start()
            down.start()

    for g in get_small:
        g.wait()
    on_diagonal = lax.broadcasted_iota(jnp.int32, (rows_dev, rows_dev), 0) == lax.broadcasted_iota(
        jnp.int32, (rows_dev, rows_dev), 1
    )
    gaps = jnp.broadcast_to(gap_row[...], (rows_dev, rows_dev))
    gap = jnp.sum(jnp.where(on_diagonal, gaps, 0.0), axis=1, keepdims=True)
    gap = jnp.broadcast_to(gap, (rows_dev, TILE))

    up.wait()
    down.wait()
    get_tiles.wait()
    first_tile = vir * tiles_dev - HT

    def ladder_step(c, carry):
        near = [amp[:, lanes((c + q) * TILE, TILE)] for q in range(2 * HT + 1)]
        tile = vir * tiles_dev + c
        at = (jnp.maximum(tile - HT, 0) - first_tile, jnp.minimum(tile + HT, 32 * tiles_dev - 1) - first_tile)
        picked = [amp[:, lanes(a * TILE, TILE)] for a in at]
        for k in range(2, KMAX):
            offset = rows[k, c] - (tile - HT)
            one = near[0]
            for q in range(1, 2 * HT + 1):
                one = jnp.where(offset == q, near[q], one)
            picked.append(jnp.where(count[c] > k, one, jnp.zeros_like(one)))
        term = jnp.dot(
            jnp.concatenate(picked, axis=1), tiles[c].reshape(KMAX * TILE, TILE),
            preferred_element_type=jnp.float32,
        )
        inverse = 1.0 / (gap + energy[pl.ds(c, 1), :])
        old = amp[:, lanes(halo + c * TILE, TILE)].astype(jnp.float32)
        scale[c] = inverse
        base[c] = old + term * inverse
        return carry

    lax.fori_loop(0, EARLY, ladder_step, 0, unroll=UNROLL)

    def forward(n, slot):
        part = weights.at[slot, mine]
        copy = pltpu.make_async_remote_copy(
            part, part, f_send.at[n], f_recv.at[n],
            device_id=(occ, partner((0, 0, 1))), device_id_type=MESH,
        )
        copy.start()
        return copy

    def product(p, n):
        w = weights[(occ + 4 - TURNS[n]) % 4]
        rhs = jnp.concatenate(
            [blocks[p, :, :, pl.ds(i * NJ, NJ), :].reshape(-1, TILE) for i in range(2)], axis=1
        )
        part = jnp.dot(w, rhs, preferred_element_type=jnp.float32)
        pair = [part[:, i * TILE:(i + 1) * TILE].reshape(32, 8, TILE) for i in range(2)]
        made[:, p, n] = jnp.concatenate(pair, axis=1).astype(jnp.bfloat16)

    def send(p, n, size):
        some = pl.ds(n, size)
        pltpu.make_async_copy(
            made.at[vir, p, some], cycle.at[vir, p, some], out_recv.at[len(STEPS)]
        ).start()
        for q, d in enumerate(STEPS):
            u = partner(d)
            pltpu.make_async_remote_copy(
                made.at[u, p, some], cycle.at[vir, p, some], out_send, out_recv.at[q],
                device_id=(occ, u), device_id_type=MESH,
            ).start()

    w_copies[0].wait()
    w_copies.append(along(before, quarters[0], 2, after))
    w_copies[2].start()
    w_copies[1].wait()
    w_copies.append(along(after, quarters[1], 3, before))
    w_copies[3].start()
    forwards = [forward(0, before), forward(1, after)]
    pltpu.make_async_copy(blocks.at[0], blocks.at[0], in_recv.at[0]).wait()
    product(0, 0)
    forwards[0].wait()
    product(0, 1)
    send(0, 0, 2)
    w_copies[2].wait()
    w_copies[3].wait()
    forwards.append(forward(2, across))
    lax.fori_loop(EARLY, EARLY + MIDDLE, ladder_step, 0, unroll=UNROLL)
    pltpu.make_async_copy(blocks.at[1], blocks.at[1], in_recv.at[1]).wait()
    product(1, 0)
    product(1, 1)
    send(1, 0, 2)
    forwards[1].wait()
    forwards[2].wait()
    for p in range(PARTS):
        product(p, 2)
        product(p, 3)
        send(p, 2, 2)

    lax.fori_loop(EARLY + MIDDLE, tiles_dev, ladder_step, 0, unroll=UNROLL)

    low = lax.broadcasted_iota(jnp.int32, (4, 8, TILE), 1) < 4
    places = []
    for o in range(4):
        s = (occ + 4 - o) % 4
        places.append(s + (s // 2) * (5 - 2 * s))
    for q, d in enumerate(STEPS + [(0, 0, 0)]):
        v = source(d)
        pltpu.make_async_copy(cycle.at[v], cycle.at[v], out_recv.at[q]).wait()
        got = [cycle[v, :, n].astype(jnp.float32).reshape(4, 8, TILE) for n in places]
        for b in range(NB_DEV):
            term = []
            for even, odd in ((got[0], got[1]), (got[2], got[3])):
                if b == 0:
                    term.append(jnp.where(low, even, pltpu.roll(odd, 4, 1)))
                else:
                    term.append(jnp.where(low, pltpu.roll(even, 4, 1), odd))
            term = jnp.stack(term, axis=1).reshape(rows_dev, TILE)
            c = b * (NA // TILE) + v
            at = lanes(c * TILE, TILE)
            result[:, at] = (base[c] + term * scale[c]).astype(jnp.bfloat16)
            pltpu.make_async_copy(result.at[:, at], out_ref.at[:, at], local_sem.at[7]).start()

    pltpu.make_async_copy(result, out_ref, local_sem.at[7]).wait()
    sent = blocks.at[:, pl.ds(0, len(STEPS))]
    pltpu.make_async_copy(sent, sent, in_send).wait()
    sent = cycle.at[pl.ds(0, len(STEPS))]
    pltpu.make_async_copy(sent, sent, out_send).wait()


def local(
    amplitudes, cycle_integrals, ladder_tiles, ladder_rows, ladder_count, row_gap, column_energy
):
    rows_dev, cols_dev = amplitudes.shape
    tiles_dev = cols_dev // TILE
    integrals = cycle_integrals.reshape(-1, cycle_integrals.shape[-1])
    bf16, f32 = jnp.bfloat16, jnp.float32
    dma = pltpu.SemaphoreType.DMA
    hbm = pl.BlockSpec(memory_space=pltpu.HBM)
    return pl.pallas_call(
        kernel,
        out_shape=jax.ShapeDtypeStruct((rows_dev, cols_dev), bf16),
        in_specs=[hbm] * 7,
        out_specs=hbm,
        scratch_shapes=[
            pltpu.VMEM((rows_dev, cols_dev + 2 * HT * TILE), bf16),
            pltpu.VMEM((PARTS, 32, NB_DEV, rows_dev // PARTS, TILE), bf16),
            pltpu.VMEM((4, 256, 1024), bf16),
            pltpu.VMEM((tiles_dev, KMAX, TILE, TILE), bf16),
            pltpu.VMEM((32, PARTS, 4, 16, TILE), bf16),
            pltpu.VMEM((32, PARTS, 4, 16, TILE), bf16),
            pltpu.VMEM((tiles_dev, rows_dev, TILE), f32),
            pltpu.VMEM((tiles_dev, rows_dev, TILE), f32),
            pltpu.VMEM(integrals.shape, bf16),
            pltpu.VMEM(integrals.shape, f32),
            pltpu.VMEM((1, rows_dev), f32),
            pltpu.VMEM((tiles_dev, TILE), f32),
            pltpu.SMEM((KMAX, tiles_dev), jnp.int32),
            pltpu.SMEM((tiles_dev,), jnp.int32),
            pltpu.VMEM((rows_dev, cols_dev), bf16),
            dma, dma((PARTS,)), dma((4,)), dma((4,)), dma((3,)), dma((3,)), dma, dma((32,)),
            dma((2,)), dma((2,)), dma((8,)),
        ],
        compiler_params=pltpu.CompilerParams(
            collective_id=0, has_side_effects=True, vmem_limit_bytes=62 * 2**20
        ),
        name="cycle_and_ladder",
    )(
        ladder_rows.T, ladder_count, amplitudes, integrals, ladder_tiles,
        row_gap.reshape(1, rows_dev), column_energy.reshape(tiles_dev, TILE),
    )


def solution(mesh):
    in_specs = (
        P("occ", "vir"),
        P(None, None, "occ", None),
        P("vir", None, None, None),
        P("vir", None),
        P("vir"),
        P("occ"),
        P("vir"),
    )
    return jax.shard_map(
        local, mesh=mesh, in_specs=in_specs, out_specs=P("occ", "vir"), check_vma=False
    )
```
